32 devices in a mesh: seq: 16 (over z, y, x), ch: 2 (over core).
Axes of the slice: x: 2, y: 2, z: 4, core: 2. Of those that a mesh axis runs over, the one named last changes fastest.
Arguments:
- seq_values: bfloat16 [1024, 512, 512], P('ch', 'seq'), may hold values from -6 to 6
- gate_values: bfloat16 [1024, 512, 512], P('ch', 'seq'), may hold values from -6 to 6
- out_grad: bfloat16 [1024, 512, 512], P('ch', 'seq'), may hold values from -6 to 6
- factor_one: bfloat16 [512, 512], replicated, may hold values from -0.25 to 0.25
- factor_two: bfloat16 [512, 512], replicated, may hold values from -0.25 to 0.25
- twiddle: bfloat16 [512, 512], P('seq'), may hold values from 0.3984375 to 1.59375
Outputs:
- values_grad: bfloat16 [1024, 512, 512], P('ch', 'seq')
- gate_grad: bfloat16 [1024, 512, 512], P('ch', 'seq')
- factor_one_grad: float32 [512, 512], P('seq')
- factor_two_grad: float32 [512, 512], P('seq')
- twiddle_grad: float32 [512, 512], P('seq')
The draws below stay inside these ranges and needn't reach their ends.
All inputs are finite; a program needn't handle non-finite values.
Results may differ from the reference program's by a relative error of at most 0.0064.
Values may be sent and summed in bfloat16 or wider, within the bound.
No kernel may reach another device: no remote copies, remote signals or barrier semaphores. Data moves between devices by JAX's collectives and lax.ppermute only.
A program may use at most 256 MiB of HBM per device.

```python
import jax
import jax.numpy as jnp
from jax import lax

D = 1024
B = 512
S = 512


def block_scale(own_key, dims, split, smallest, top_value):
    level, own = 1.0, jax.random.fold_in(own_key, 6)
    for axis_at, shards_of in split:
        draws = jnp.exp(jax.random.uniform(jax.random.fold_in(own, axis_at), (shards_of,), jnp.float32, smallest / len(split), top_value / len(split)))
        level = level * jnp.repeat(draws, dims[axis_at] // shards_of).reshape([-1 if axis == axis_at else 1 for axis in range(len(dims))])
    return level


def normal_values(stream_key, shape, spread, limit, pieces=(), dtype=jnp.bfloat16):
    result = spread * jax.random.normal(stream_key, shape, jnp.float32)
    if pieces:
        result = result * block_scale(stream_key, shape, pieces, -0.22, 0.18)
    return jnp.clip(result, -limit, limit).astype(dtype)


def setup_inputs(seed: int = 0) -> dict:
    seeds = jax.random.split(jax.random.key(seed), 7)
    return {
        "seq_values": normal_values(seeds[0], (D, B, S), 1.0, 6.0, ((0, 2), (1, 16))),
        "gate_values": normal_values(seeds[1], (D, B, S), 1.0, 6.0, ((0, 2), (1, 16))),
        "out_grad": normal_values(seeds[2], (D, B, S), 1.0, 6.0, ((0, 2), (1, 16))),
        "factor_one": normal_values(seeds[3], (S, S), S ** -0.5, 0.25),
        "factor_two": normal_values(seeds[4], (B, B), B ** -0.5, 0.25),
        "twiddle": jnp.clip(0.3984375 + 1.1953125 * jax.random.uniform(seeds[5], (B, S), jnp.float32) ** block_scale(seeds[5], (B, S), ((0, 16),), -0.2, 0.2), 0.3984375, 1.59375).astype(jnp.bfloat16),
    }


def reference(seq_values, gate_values, out_grad, factor_one, factor_two, twiddle):
    group = 16
    f32 = jnp.float32
    first = factor_one.astype(f32)
    second = factor_two.astype(f32)
    twiddle_f = twiddle.astype(f32)
    shape = (D // group, group, B, S)
    stacked = (seq_values.reshape(shape), gate_values.reshape(shape), out_grad.reshape(shape))

    def step(carry, items):
        first_sum, second_sum, twiddle_sum = carry
        values, gates, grads = items
        values_f = values.astype(f32)
        pre_twiddle = jnp.einsum('cbs,rs->cbr', values_f, first)
        mixed_first = (pre_twiddle * twiddle_f[None]).astype(jnp.bfloat16)
        mixed = jnp.einsum('cbr,jb->cjr', mixed_first.astype(f32), second).astype(jnp.bfloat16)
        gate_grad = (grads.astype(f32) * mixed.astype(f32)).astype(jnp.bfloat16)
        mixed_grad = (gates.astype(f32) * grads.astype(f32)).astype(jnp.bfloat16)
        mixed_grad_f = mixed_grad.astype(f32)
        first_grad = jnp.einsum('cjr,jb->cbr', mixed_grad_f, second).astype(jnp.bfloat16)
        second_sum = second_sum + jnp.einsum('cjr,cbr->jb', mixed_grad_f, mixed_first.astype(f32))
        first_grad_f = first_grad.astype(f32)
        scaled_grad = (first_grad_f * twiddle_f[None]).astype(jnp.bfloat16)
        twiddle_sum = twiddle_sum + jnp.sum(first_grad_f * pre_twiddle, axis=0)
        scaled_f = scaled_grad.astype(f32)
        values_grad = jnp.einsum('cbr,rs->cbs', scaled_f, first).astype(jnp.bfloat16)
        first_sum = first_sum + jnp.einsum('cbr,cbs->rs', scaled_f, values_f)
        return (first_sum, second_sum, twiddle_sum), (values_grad, gate_grad)

    init = (jnp.zeros((S, S), f32), jnp.zeros((B, B), f32), jnp.zeros((B, S), f32))
    sums, grads_out = lax.scan(step, init, stacked)
    first_sum, second_sum, twiddle_sum = sums
    values_grad = grads_out[0].reshape(D, B, S)
    gate_grad = grads_out[1].reshape(D, B, S)
    factor_one_grad = first_sum * (1.0 / (D * B) ** 0.5)
    factor_two_grad = second_sum * (1.0 / (D * S) ** 0.5)
    twiddle_grad = twiddle_sum * (1.0 / D ** 0.5)
    return (values_grad, gate_grad, factor_one_grad, factor_two_grad, twiddle_grad)
```

```python
import math

import jax
import jax.numpy as jnp
from jax import lax
from jax.experimental import pallas as pl
from jax.experimental.pallas import tpu as pltpu
from jax.sharding import PartitionSpec as P

f32 = jnp.float32
bf16 = jnp.bfloat16


def dot(a, b, dims):
    return lax.dot_general(a, b, (dims, ((), ())), preferred_element_type=f32)


def first_kernel(x_ref, f1_ref, tw_ref, out_ref):
    p, n, b, s = x_ref.shape
    pre = dot(x_ref[...].reshape(p * n * b, s), f1_ref[...], ((1,), (1,)))
    out = pre.reshape(p * n, b, -1) * tw_ref[...].astype(f32)[None]
    out_ref[...] = out.astype(bf16).reshape(p, n, b, s)


def product_kernel(g_ref, o_ref, out_ref):
    out_ref[...] = (g_ref[...].astype(f32) * o_ref[...].astype(f32)).astype(bf16)


def mix_grad_kernel(g_ref, f2t_ref, out_ref):
    a, n, b, s = g_ref.shape
    for i in range(n):
        got = dot(f2t_ref[...], g_ref[:, i].reshape(a * b, s), ((1,), (0,)))
        out_ref[:, i] = got.astype(bf16).reshape(a, b, s)


def at_start():
    return (pl.program_id(0) == 0) & (pl.program_id(1) == 0)


def mix_kernel(v_ref, g_ref, f2_ref, out_ref, sum_ref):
    a, n, b, s = v_ref.shape

    @pl.when(at_start())
    def _():
        sum_ref[...] = jnp.zeros(sum_ref.shape, f32)

    for i in range(n):
        vals = v_ref[:, i].reshape(a * b, s)
        out_ref[:, i] = dot(f2_ref[...], vals, ((1,), (0,))).astype(bf16).reshape(a, b, s)
        sum_ref[...] += dot(g_ref[:, i].reshape(a * b, s), vals, ((1,), (1,)))


def last_kernel(d_ref, x_ref, f1_ref, tw_ref, out_ref, one_ref, tw_sum_ref):
    p, n, b, s = x_ref.shape

    @pl.when(at_start())
    def _():
        one_ref[...] = jnp.zeros(one_ref.shape, f32)
        tw_sum_ref[...] = jnp.zeros(tw_sum_ref.shape, f32)

    x = x_ref[...].reshape(p * n * b, s)
    pre = dot(x, f1_ref[...], ((1,), (1,))).reshape(p * n, b, -1)
    grad = d_ref[...].astype(f32).reshape(p * n, b, -1)
    tw_sum_ref[...] += jnp.sum(grad * pre, axis=0)
    scaled = (grad * tw_ref[...].astype(f32)[None]).astype(bf16).reshape(p * n * b, -1)
    out_ref[...] = dot(scaled, f1_ref[...], ((1,), (0,))).astype(bf16).reshape(p, n, b, s)
    one_ref[...] += dot(scaled, x, ((0,), (0,)))


def stage(name, kernel, unit, peers, count, reads, small, write, sums=()):
    size, _, b, s = reads[0][0].shape
    peers = math.gcd(size, peers)

    def part(first):
        return pl.BlockSpec((peers, unit, b, s), lambda p, i: (p, first // unit + i, 0, 0))

    def whole(shape):
        return pl.BlockSpec(shape, lambda p, i: (0,) * len(shape))

    into, slots, first = write
    operands = [v for v, _ in reads] + list(small)
    specs = [part(at) for _, at in reads] + [whole(v.shape) for v in small]
    fixed = len(operands)
    alias = {}
    call = kernel
    if into is not None:
        alias = {fixed: 0}
        operands.append(into)
        specs.append(pl.BlockSpec(memory_space=pl.ANY))

        def call(*refs):
            kernel(*refs[:fixed], *refs[fixed + 1 :])

    out = pl.pallas_call(
        call,
        grid=(size // peers, count // unit),
        in_specs=specs,
        out_specs=[part(first)] + [whole(v) for v in sums],
        out_shape=[jax.ShapeDtypeStruct((size, slots, b, s), bf16)]
        + [jax.ShapeDtypeStruct(v, f32) for v in sums],
        input_output_aliases=alias,
        name=name,
    )(*operands)
    return out if sums else out[0]


def halve(parts, bit):
    size = lax.axis_size("seq")
    axis = parts.ndim - 3
    own = (lax.axis_index("seq") >> bit) & 1
    keep = lax.dynamic_index_in_dim(parts, own, axis, keepdims=False)
    send = lax.dynamic_index_in_dim(parts, 1 - own, axis, keepdims=False)
    pairs = [(i, i ^ (1 << bit)) for i in range(size)]
    return keep + lax.ppermute(send, "seq", pairs)


def scatter_sum(total, beside=None):
    size = lax.axis_size("seq")
    bits = size.bit_length() - 1
    rows = total.shape[0] // size
    parts = total.reshape((2,) * bits + (rows, total.shape[1]))
    for bit in range(bits):
        parts = halve(parts, bit)
        if bit == 0 and beside is not None:
            parts, beside = lax.optimization_barrier((parts, beside))
    return parts, beside


def channel_sum(value):
    size = lax.axis_size("ch")
    step = 1
    while step < size:
        value = value + lax.ppermute(value, "ch", [(i, i ^ step) for i in range(size)])
        step *= 2
    return value


def body(x, gate, og, f1, f2, tw):
    size = lax.axis_size("seq")
    own_width, b, s = x.shape
    width = own_width * lax.axis_size("ch")
    blocks = f2.shape[0]
    slots = own_width // size
    bounds = [0, max(1, slots // 8), slots // 2, slots]
    unit = math.gcd(*bounds, 4)
    counts = [hi - lo for lo, hi in zip(bounds, bounds[1:])]
    by_peer = lambda v: v.reshape(size, slots, b, s)
    x, gate, og = by_peer(x), by_peer(gate), by_peer(og)
    f2t = f2.T
    got = {}
    two_parts = []

    def make(kind, k, write):
        count, at = counts[k], bounds[k]
        if kind == "A":
            return stage("grad", product_kernel, unit, 8, count, [(gate, at), (og, at)], [], write)
        if kind == "B":
            return stage("first", first_kernel, unit, 4, count, [(x, at)], [f1, tw], write)
        if kind == "D":
            return stage("mix_grad", mix_grad_kernel, unit, size, count, [got["A", k]], [f2t], write)
        out, part = stage(
            "mix", mix_kernel, unit, size, count, [got["B", k], got["A", k]], [f2], write, [f2.shape]
        )
        two_parts.append(part)
        return out

    token = None
    two_rows = None
    plan = [
        [("A", 0)],
        [("B", 0), ("B", 1), ("A", 1), ("A", 2)],
        [("D", 0), ("B", 2)],
        [("D", 1), ("D", 2), ("C", 0), ("C", 1)],
        [("C", 2)],
    ]
    for piece in plan:
        total = sum(counts[k] for _, k in piece)
        buffer, first, places = None, 0, []
        for kind, k in piece:
            buffer = make(kind, k, (buffer, total, first))
            places.append((kind, k, first))
            first += counts[k]
        if len(two_parts) == len(counts) and two_rows is None:
            two_rows, _ = scatter_sum(sum(two_parts[1:], two_parts[0]))
            buffer, token, two_rows = lax.optimization_barrier((buffer, token, two_rows))
        elif token is not None:
            buffer, token = lax.optimization_barrier((buffer, token))
        token = lax.all_to_all(
            buffer.reshape(-1, b, s), "seq", split_axis=0, concat_axis=0, tiled=True
        )
        here = token.reshape(size, total, b, s)
        for kind, k, first in places:
            got[kind, k] = (here, first)

    values_grad = gate_grad = None
    one_parts, tw_parts = [], []
    for k, (at, count) in enumerate(zip(bounds, counts)):
        values_grad, one, tw_part = stage(
            "last", last_kernel, unit, 4, count, [got["D", k], (x, at)], [f1, tw],
            (values_grad, slots, at), [f1.shape, tw.shape],
        )
        one_parts.append(one)
        tw_parts.append(tw_part)
    for k in (0, 1):
        gate_grad = stage(
            "gate", product_kernel, unit, 8, counts[k], [got["C", k], (og, bounds[k])], [],
            (gate_grad, slots, bounds[k]),
        )
    one_rows, gate_grad = scatter_sum(sum(one_parts[1:], one_parts[0]), gate_grad)
    tw_rows = sum(tw_parts[1:], tw_parts[0])
    one_rows, two_rows, tw_rows = channel_sum(jnp.stack([one_rows, two_rows, tw_rows]))
    gate_grad = stage(
        "gate", product_kernel, unit, 8, counts[2], [got["C", 2], (og, bounds[2])], [],
        (gate_grad, slots, bounds[2]),
    )
    return (
        values_grad.reshape(own_width, b, s),
        gate_grad.reshape(own_width, b, s),
        one_rows * (1.0 / (width * blocks) ** 0.5),
        two_rows * (1.0 / (width * s) ** 0.5),
        tw_rows * (1.0 / width**0.5),
    )


def solution(mesh):
    return jax.shard_map(
        body,
        mesh=mesh,
        in_specs=(
            P("ch", "seq", None),
            P("ch", "seq", None),
            P("ch", "seq", None),
            P(),
            P(),
            P("seq", None),
        ),
        out_specs=(
            P("ch", "seq", None),
            P("ch", "seq", None),
            P("seq", None),
            P("seq", None),
            P("seq", None),
        ),
        check_vma=False,
    )
```

```python
import math

import jax
import jax.numpy as jnp
from jax import lax
from jax.experimental import pallas as pl
from jax.experimental.pallas import tpu as pltpu
from jax.sharding import PartitionSpec as P


f32 = jnp.float32
bf16 = jnp.bfloat16
LINE = 4
CHUNKS = 2


def dot(a, b, dims):
    return lax.dot_general(a, b, (dims, ((), ())), preferred_element_type=f32)


def first_kernel(x_ref, f1_ref, tw_ref, out_ref):
    p, n, b, s = x_ref.shape
    pre = dot(x_ref[...].reshape(p * n * b, s), f1_ref[...], ((1,), (1,)))
    out = pre.reshape(p * n, b, -1) * tw_ref[...].astype(f32)[None]
    out_ref[...] = out.astype(bf16).reshape(p, n, b, s)


def product_kernel(g_ref, o_ref, out_ref):
    out_ref[...] = (g_ref[...].astype(f32) * o_ref[...].astype(f32)).astype(bf16)


def at_start():
    return (pl.program_id(0) == 0) & (pl.program_id(1) == 0)


def rows_of(refs, i):
    return jnp.concatenate([r[:, i].reshape(-1, r.shape[-1]) for r in refs], axis=0)


def write_rows(refs, i, value):
    step = value.shape[0] // len(refs)
    for k, r in enumerate(refs):
        r[:, i] = value[k * step : (k + 1) * step].reshape(r.shape[0], *r.shape[2:])


def mix_grad_kernel(*refs):
    grads, f2t_ref, outs = refs[:LINE], refs[LINE], refs[LINE + 1 :]
    for i in range(grads[0].shape[1]):
        write_rows(outs, i, dot(f2t_ref[...], rows_of(grads, i), ((1,), (0,))).astype(bf16))


def mix_kernel(*refs):
    vals, grads, f2_ref = refs[:LINE], refs[LINE : 2 * LINE], refs[2 * LINE]
    outs, sum_ref = refs[2 * LINE + 1 : -1], refs[-1]

    @pl.when(pl.program_id(0) == 0)
    def _():
        sum_ref[...] = jnp.zeros(sum_ref.shape, f32)

    for i in range(vals[0].shape[1]):
        v = rows_of(vals, i)
        write_rows(outs, i, dot(f2_ref[...], v, ((1,), (0,))).astype(bf16))
        sum_ref[...] += dot(rows_of(grads, i), v, ((1,), (1,)))


def last_kernel(d_ref, x_ref, f1_ref, tw_ref, out_ref, one_ref, tw_sum_ref):
    p, n, b, s = x_ref.shape

    @pl.when(at_start())
    def _():
        one_ref[...] = jnp.zeros(one_ref.shape, f32)
        tw_sum_ref[...] = jnp.zeros(tw_sum_ref.shape, f32)

    x = x_ref[...].reshape(p * n * b, s)
    pre = dot(x, f1_ref[...], ((1,), (1,))).reshape(p * n, b, -1)
    grad = d_ref[...].astype(f32).reshape(p * n, b, -1)
    tw_sum_ref[...] += jnp.sum(grad * pre, axis=0)
    scaled = (grad * tw_ref[...].astype(f32)[None]).astype(bf16).reshape(p * n * b, -1)
    out_ref[...] = dot(scaled, f1_ref[...], ((1,), (0,))).astype(bf16).reshape(p, n, b, s)
    one_ref[...] += dot(scaled, x, ((0,), (0,)))


def mid_stage(kernel, slabs, factor, sums=()):
    g, count, b, s = slabs[0].shape
    unit = math.gcd(count, 4)
    part = pl.BlockSpec((g, unit, b, s), lambda i: (0, i, 0, 0))
    whole = lambda shape: pl.BlockSpec(shape, lambda i: (0, 0))
    out = pl.pallas_call(
        kernel,
        grid=(count // unit,),
        in_specs=[part] * len(slabs) + [whole(factor.shape)],
        out_specs=[part] * LINE + [whole(v) for v in sums],
        out_shape=[jax.ShapeDtypeStruct(slabs[0].shape, bf16)] * LINE
        + [jax.ShapeDtypeStruct(v, f32) for v in sums],
    )(*slabs, factor)
    return list(out[:LINE]), list(out[LINE:])


def stage(kernel, most, line, lo, slab, count, wide, small, into=False, sums=()):
    size, slots, b, s = wide[0].shape
    g = size // LINE
    unit = math.gcd(count, lo, most)
    at = lambda one, i, z: (z[0], lo // unit + i, 0, 0)
    own = lambda one, i, z: (0, i, 0, 0)
    block = (g, unit, b, s)
    whole = lambda shape: pl.BlockSpec(shape, lambda one, i, z: (0,) * len(shape))
    operands = ([] if slab is None else [slab]) + list(wide) + list(small)
    specs = [] if slab is None else [pl.BlockSpec(block, own)]
    specs += [pl.BlockSpec(block, at) for _ in wide] + [whole(v.shape) for v in small]
    fixed = len(operands)
    alias = {}
    aliased = into is not None and into is not False
    if aliased:
        alias = {fixed + 1: 0}
        operands.append(into)
        specs.append(pl.BlockSpec(memory_space=pl.ANY))

    def call(z_ref, *refs):
        kernel(*refs[:fixed], *refs[fixed + aliased :])

    shape = (g, count, b, s) if into is False else (size, slots, b, s)
    out = pl.pallas_call(
        call,
        grid_spec=pltpu.PrefetchScalarGridSpec(
            num_scalar_prefetch=1,
            grid=(1, count // unit),
            in_specs=specs,
            out_specs=[pl.BlockSpec(block, own if into is False else at)]
            + [whole(v) for v in sums],
        ),
        out_shape=[jax.ShapeDtypeStruct(shape, bf16)]
        + [jax.ShapeDtypeStruct(v, f32) for v in sums],
        input_output_aliases=alias,
    )(line.reshape(1), *operands)
    return out if sums else out[0]


def scatter_sum(total):
    size = lax.axis_size("seq")
    bits = size.bit_length() - 1
    rows = total.shape[0] // size
    parts = total.reshape((2,) * bits + (rows, total.shape[1]))
    for bit in range(bits):
        axis = parts.ndim - 3
        own = (lax.axis_index("seq") >> bit) & 1
        keep = lax.dynamic_index_in_dim(parts, own, axis, keepdims=False)
        send = lax.dynamic_index_in_dim(parts, 1 - own, axis, keepdims=False)
        pairs = [(i, i ^ (1 << bit)) for i in range(size)]
        parts = keep + lax.ppermute(send, "seq", pairs)
    return parts


def channel_sum(value):
    size = lax.axis_size("ch")
    step = 1
    while step < size:
        value = value + lax.ppermute(value, "ch", [(i, i ^ step) for i in range(size)])
        step *= 2
    return value


def add_all(parts):
    return sum(parts[1:], parts[0])


def body(x, gate, og, f1, f2, tw):
    size = lax.axis_size("seq")
    g = size // LINE
    own_width, b, s = x.shape
    width = own_width * lax.axis_size("ch")
    blocks = f2.shape[0]
    slots = own_width // size
    by_peer = lambda v: v.reshape(size, slots, b, s)
    x, gate, og = by_peer(x), by_peer(gate), by_peer(og)
    count = slots // CHUNKS
    starts = [k * count for k in range(CHUNKS)]
    place = lax.axis_index("seq") // g
    lines = [place ^ k for k in range(LINE)]
    order = jnp.stack(lines)

    def reorder(m):
        m = m.reshape(LINE, -1, m.shape[1])[order].reshape(m.shape)
        return m.reshape(m.shape[0], LINE, -1)[:, order].reshape(m.shape)

    f2r = reorder(f2)
    f2rt = f2r.T
    groups = [[i * g + j for j in range(g)] for i in range(LINE)]

    def across(slabs):
        out = [slabs[0]] + [None] * (LINE - 1)
        for k in range(LINE - 1, 0, -1):
            out[k] = lax.ppermute(slabs[k], "seq", [(i, i ^ (k * g)) for i in range(size)])
        return out

    def within(slabs):
        return [
            lax.all_to_all(
                v.reshape(-1, b, s), "seq", 0, 0, axis_index_groups=groups, tiled=True
            ).reshape(v.shape)
            for v in slabs
        ]

    def grads_of(lo):
        return [stage(product_kernel, 8, z, lo, None, count, [gate, og], []) for z in lines]

    def firsts_of(lo):
        return [stage(first_kernel, 4, z, lo, None, count, [x], [f1, tw]) for z in lines]

    over = [across(grads_of(lo)) for lo in starts]
    vals_over = [across(firsts_of(lo)) for lo in starts]
    d_got, c_got, two_parts = [], [], []
    for c in range(CHUNKS):
        over[c] = within(over[c])
        made = mid_stage(mix_grad_kernel, over[c], f2rt)[0]
        d_got.append(across(within(made)))
    for c in range(CHUNKS):
        vals = within(vals_over[c])
        mixed, parts = mid_stage(mix_kernel, vals + over[c], f2r, [f2.shape])
        two_parts += parts
        c_got.append(across(within(mixed)))
    two_sum = reorder(add_all(two_parts))

    values_grad = gate_grad = None
    one_parts, tw_parts = [], []
    for lo, d in zip(starts, d_got):
        for z, slab in zip(lines, d):
            values_grad, one, tw_part = stage(
                last_kernel, 4, z, lo, slab, count, [x], [f1, tw], values_grad,
                [f1.shape, tw.shape],
            )
            one_parts.append(one)
            tw_parts.append(tw_part)
    rows = scatter_sum(jnp.concatenate([add_all(one_parts), two_sum], axis=1))
    sums = channel_sum(jnp.concatenate([rows, add_all(tw_parts)], axis=1))
    for lo, c in zip(starts, c_got):
        for z, slab in zip(lines, c):
            gate_grad = stage(product_kernel, 8, z, lo, slab, count, [og], [], gate_grad)
    one_rows = sums[:, :s]
    two_rows = sums[:, s : s + blocks]
    tw_rows = sums[:, s + blocks :]
    return (
        values_grad.reshape(own_width, b, s),
        gate_grad.reshape(own_width, b, s),
        one_rows * (1.0 / (width * blocks) ** 0.5),
        two_rows * (1.0 / (width * s) ** 0.5),
        tw_rows * (1.0 / width**0.5),
    )


def solution(mesh):
    return jax.shard_map(
        body,
        mesh=mesh,
        in_specs=(
            P("ch", "seq", None),
            P("ch", "seq", None),
            P("ch", "seq", None),
            P(),
            P(),
            P("seq", None),
        ),
        out_specs=(
            P("ch", "seq", None),
            P("ch", "seq", None),
            P("seq", None),
            P("seq", None),
            P("seq", None),
        ),
        check_vma=False,
    )
```
